32 devices in a mesh: grp: 4 (over x, core), seq: 8 (over z, y).
Axes of the slice: x: 2, y: 2, z: 4, core: 2. Of those that a mesh axis runs over, the one named last changes fastest.
Arguments:
- tokens: bfloat16 [8, 2048, 1024], P('grp', 'seq'), may hold values from -6 to 6
- offsets: int32 [8, 8], P('grp'), may hold values from 256 to 1024, as said below
- query_head_weight: bfloat16 [1024, 96], P(('grp', 'seq')), may hold values from -0.4375 to 0.4375
- query_dim_weight: bfloat16 [1024, 384], P(('grp', 'seq')), may hold values from -0.1875 to 0.1875
- key_head_weight: bfloat16 [1024, 32], P(('grp', 'seq')), may hold values from -0.375 to 0.375
- key_dim_weight: bfloat16 [1024, 128], P(('grp', 'seq')), may hold values from -0.1875 to 0.1875
- value_head_weight: bfloat16 [1024, 32], P(('grp', 'seq')), may hold values from -0.1875 to 0.1875
- value_dim_weight: bfloat16 [1024, 128], P(('grp', 'seq')), may hold values from -0.1875 to 0.1875
- out_weight: bfloat16 [1024, 1024], P(('grp', 'seq')), may hold values from -0.75 to 0.75
- attention_gain: bfloat16 [1024], P(('grp', 'seq')), may hold values from 0.5 to 1.5
- gate_weight: bfloat16 [1024, 2816], P(('grp', 'seq')), may hold values from -0.1875 to 0.1875
- up_weight: bfloat16 [1024, 2816], P(('grp', 'seq')), may hold values from -0.1875 to 0.1875
- down_weight: bfloat16 [2816, 1024], P(('grp', 'seq')), may hold values from -0.109375 to 0.109375
- feedforward_gain: bfloat16 [1024], P(('grp', 'seq')), may hold values from 0.5 to 1.5
- cotangent: bfloat16 [8, 2048, 1024], P('grp', 'seq'), may hold values from -6 to 6
Outputs:
- output: bfloat16 [8, 2048, 1024], P('grp', 'seq')
- input_gradient: bfloat16 [8, 2048, 1024], P('grp', 'seq')
- query_head_gradient: float32 [1024, 96], P(('grp', 'seq'))
- query_dim_gradient: float32 [1024, 384], P(('grp', 'seq'))
- key_head_gradient: float32 [1024, 32], P(('grp', 'seq'))
- key_dim_gradient: float32 [1024, 128], P(('grp', 'seq'))
- value_head_gradient: float32 [1024, 32], P(('grp', 'seq'))
- value_dim_gradient: float32 [1024, 128], P(('grp', 'seq'))
- out_gradient: float32 [1024, 1024], P(('grp', 'seq'))
- attention_gain_gradient: float32 [1024], P(('grp', 'seq'))
- gate_gradient: float32 [1024, 2816], P(('grp', 'seq'))
- up_gradient: float32 [1024, 2816], P(('grp', 'seq'))
- down_gradient: float32 [2816, 1024], P(('grp', 'seq'))
- feedforward_gain_gradient: float32 [1024], P(('grp', 'seq'))
The draws below stay inside these ranges and needn't reach their ends.
Inputs may be any that keep to these rules, and one draw needn't show every extreme that they name: `offsets`: in every group one continuation follows the whole prompt and another follows its first 256 tokens; the others follow 1024 // 4 to 1024 tokens.
All inputs are finite; a program needn't handle non-finite values.
Results may differ from the reference program's by a relative error of at most 0.035.
Values may be sent and summed in bfloat16 or wider, within the bound.
No kernel may reach another device: no remote copies, remote signals or barrier semaphores. Data moves between devices by JAX's collectives and lax.ppermute only.
A program may use at most 192 MiB of HBM per device.

```python
import jax
import jax.numpy as jnp
from jax import lax

D = 1024
H = 16
HD = 64
RQ = 6
RK = 2
FF = 2816
PROMPT = 1024
CONT = 128
NCONT = 8
SEQLEN = 2048
GROUPS = 8


def draw_offsets(key, part):
    base_offsets = jax.random.randint(jax.random.fold_in(key, 11), (GROUPS, NCONT), PROMPT // 4, PROMPT + 1)
    first_slot = jax.random.randint(jax.random.fold_in(key, 12), (GROUPS, 1), 0, NCONT)
    second = (first_slot + jax.random.randint(jax.random.fold_in(key, 13), (GROUPS, 1), 1, NCONT)) % NCONT
    slot_index = jnp.arange(NCONT)[None, :]
    chosen = jnp.where(slot_index == first_slot, PROMPT, base_offsets)
    return jnp.where(slot_index == second, PROMPT // 4, chosen).astype(jnp.int32)


def levels(rng, shape, pieces, low, high):
    loudness = 1.0
    for dim, shards_of in pieces:
        heights = jax.random.uniform(jax.random.fold_in(jax.random.fold_in(rng, 6), dim), (shards_of,), jnp.float32, low / len(pieces), high / len(pieces))
        loudness = loudness * jnp.repeat(jnp.exp(heights), shape[dim] // shards_of).reshape((-1,) + (1,) * (len(shape) - 1 - dim))
    return loudness


def normal_values(rng, dims, scale, bound, cuts=(), kind=jnp.bfloat16):
    values = scale * jax.random.normal(rng, dims, jnp.float32)
    if cuts:
        values = values * levels(rng, dims, cuts, -0.22, 0.18)
    return jnp.clip(values, -bound, bound).astype(kind)


def setup_inputs(seed: int = 0) -> dict:
    key_list = jax.random.split(jax.random.key(seed), 16)
    return {
        "tokens": normal_values(key_list[0], (GROUPS, SEQLEN, D), 1.0, 6.0, ((0, 4), (1, 8))),
        "offsets": draw_offsets(jax.random.fold_in(key_list[15], 71), 0),
        "query_head_weight": normal_values(key_list[2], (D, RQ * H), (D // RQ) ** -0.5, 0.4375, ((0, 32),)),
        "query_dim_weight": normal_values(key_list[3], (D, RQ * HD), D ** -0.5, 0.1875, ((0, 32),)),
        "key_head_weight": normal_values(key_list[4], (D, RK * H), (D // (2 * RK)) ** -0.5, 0.375, ((0, 32),)),
        "key_dim_weight": normal_values(key_list[5], (D, RK * HD), D ** -0.5, 0.1875, ((0, 32),)),
        "value_head_weight": normal_values(key_list[6], (D, RK * H), D ** -0.5, 0.1875, ((0, 32),)),
        "value_dim_weight": normal_values(key_list[7], (D, RK * HD), D ** -0.5, 0.1875, ((0, 32),)),
        "out_weight": normal_values(key_list[8], (H * HD, D), HD ** -0.5, 0.75, ((0, 32),)),
        "attention_gain": jnp.clip(1.0 + 0.1 * jax.random.normal(key_list[9], (D,), jnp.float32), 0.5, 1.5).astype(jnp.bfloat16),
        "gate_weight": normal_values(key_list[10], (D, FF), D ** -0.5, 0.1875, ((0, 32),)),
        "up_weight": normal_values(key_list[11], (D, FF), D ** -0.5, 0.1875, ((0, 32),)),
        "down_weight": normal_values(key_list[12], (FF, D), FF ** -0.5, 0.109375, ((0, 32),)),
        "feedforward_gain": jnp.clip(1.0 + 0.1 * jax.random.normal(key_list[13], (D,), jnp.float32), 0.5, 1.5).astype(jnp.bfloat16),
        "cotangent": normal_values(key_list[14], (GROUPS, SEQLEN, D), 1.0, 6.0, ((0, 4), (1, 8))),
    }


eps = 1e-06
highest = lax.Precision.HIGHEST

@jax.custom_vjp
def low(v):
    return lax.optimization_barrier(v.astype(jnp.bfloat16)).astype(jnp.float32)

@jax.custom_vjp
def low_back(v):
    return v

def low_keep(v):
    return (low(v), None)

def low_pass(kept, grad):
    return (grad,)

def back_keep(v):
    return (v, None)

def back_low(kept, grad):
    return (low(grad),)
low.defvjp(low_keep, low_pass)
low_back.defvjp(back_keep, back_low)

def rotate(values, positions):
    half_width = values.shape[-1] // 2
    frequency = 10000.0 ** (-2.0 * jnp.arange(half_width, dtype=jnp.float32) / values.shape[-1])
    angles = positions.astype(jnp.float32)[:, None] * frequency[None, :]
    cosine = jnp.cos(angles)[:, None, :]
    sine_part = jnp.sin(angles)[:, None, :]
    first_half = values[..., :half_width]
    second_half = values[..., half_width:]
    return jnp.concatenate([first_half * cosine - second_half * sine_part, second_half * cosine + first_half * sine_part], axis=-1)

def rms_norm(values, gain):
    return values * lax.rsqrt(lax.optimization_barrier(jnp.mean(values * values, axis=-1, keepdims=True)) + eps) * gain

def layer_group(tokens_group, offsets_group, weights):
    query_head, query_dim, key_head, key_dim, value_head, value_dim, out_proj, attention_gain, gate_proj, up_proj, down_proj, feedforward_gain = weights
    seq_length = tokens_group.shape[0]
    places = jnp.arange(seq_length, dtype=jnp.int32)
    in_continuation = places >= PROMPT
    branch_index = jnp.where(in_continuation, (places - PROMPT) // CONT, 0).astype(jnp.int32)
    branch_start = offsets_group[branch_index]
    positions = jnp.where(in_continuation, branch_start + (places - PROMPT) % CONT, places)
    query_place = places[:, None]
    key_place = places[None, :]
    key_prompt = key_place < PROMPT
    query_branch = in_continuation[:, None]
    prompt_ok = key_prompt & jnp.where(query_branch, key_place < branch_start[:, None], key_place <= query_place)
    branch_ok = ~key_prompt & query_branch & (branch_index[:, None] == branch_index[None, :]) & (key_place <= query_place)
    allowed = prompt_ok | branch_ok
    normed = low(rms_norm(tokens_group, attention_gain))

    def project(matrix):
        return jnp.dot(normed, matrix, precision=highest)
    a_query = low_back(project(query_head)).reshape(seq_length, RQ, H)
    b_query = rotate(low_back(project(query_dim)).reshape(seq_length, RQ, HD), positions)
    a_key = low(low_back(project(key_head))).reshape(seq_length, RK, H)
    b_key = low(rotate(low_back(project(key_dim)).reshape(seq_length, RK, HD), positions))
    a_value = low(low_back(project(value_head))).reshape(seq_length, RK, H)
    b_value = low(low_back(project(value_dim))).reshape(seq_length, RK, HD)
    query = low(jnp.einsum('srh,srd->shd', a_query, b_query, precision=highest) / RQ)
    keys = low(jnp.einsum('srh,srd->shd', a_key, b_key, precision=highest) / RK)
    values = low(jnp.einsum('srh,srd->shd', a_value, b_value, precision=highest) / RK)
    scores = low_back(jnp.einsum('qhd,khd->hqk', query, keys, precision=highest)) * HD ** (-0.5)
    scores = jnp.where(allowed[None], scores, -1e+30)
    top_score = lax.optimization_barrier(jnp.max(scores, axis=-1, keepdims=True))
    exponential = jnp.exp(scores - top_score)
    probabilities = low(exponential / lax.optimization_barrier(jnp.sum(exponential, axis=-1, keepdims=True)))
    mixed = low(low_back(jnp.einsum('hqk,khd->qhd', probabilities, values, precision=highest))).reshape(seq_length, H * HD)
    middle = tokens_group + low_back(jnp.dot(mixed, out_proj, precision=highest))
    normed_second = low(rms_norm(middle, feedforward_gain))
    gate = low_back(jnp.dot(normed_second, gate_proj, precision=highest))
    upper = low_back(jnp.dot(normed_second, up_proj, precision=highest))
    hidden = low(gate * jax.nn.sigmoid(gate) * upper)
    return middle + low_back(jnp.dot(hidden, down_proj, precision=highest))

def reference(tokens, offsets, query_head_weight, query_dim_weight, key_head_weight, key_dim_weight, value_head_weight, value_dim_weight, out_weight, attention_gain, gate_weight, up_weight, down_weight, feedforward_gain, cotangent):
    weights = tuple((matrix.astype(jnp.float32) for matrix in (query_head_weight, query_dim_weight, key_head_weight, key_dim_weight, value_head_weight, value_dim_weight, out_weight, attention_gain, gate_weight, up_weight, down_weight, feedforward_gain)))
    tokens_float = tokens.astype(jnp.float32)
    cotangent_float = cotangent.astype(jnp.float32)

    def forward(inputs, params):

        def one_group(pair):
            return layer_group(pair[0], pair[1], params)
        return lax.map(jax.checkpoint(one_group), (inputs, offsets))
    result, pullback = jax.vjp(forward, tokens_float, weights)
    input_grad, weight_grads = pullback(cotangent_float)
    return (result.astype(jnp.bfloat16), input_grad.astype(jnp.bfloat16), weight_grads[0], weight_grads[1], weight_grads[2], weight_grads[3], weight_grads[4], weight_grads[5], weight_grads[6], weight_grads[7], weight_grads[8], weight_grads[9], weight_grads[10], weight_grads[11])
```

```python
import jax
import jax.numpy as jnp
from jax import lax
from jax.sharding import PartitionSpec as P

D = 1024
H = 16
HD = 64
RQ = 6
RK = 2
PROMPT = 1024
CONT = 128
NCONT = 8
SEQLEN = 2048


eps = 1e-06
masked_score = -1e30


def rotate(values, positions, direction):
    half_width = values.shape[-1] // 2
    frequency = 10000.0 ** (-2.0 * jnp.arange(half_width, dtype=jnp.float32) / values.shape[-1])
    angles = positions.astype(jnp.float32)[:, None] * frequency[None, :]
    cosine = jnp.cos(angles)[:, None, :]
    sine_part = direction * jnp.sin(angles)[:, None, :]
    first_half = values[..., :half_width]
    second_half = values[..., half_width:]
    return jnp.concatenate(
        [
            first_half * cosine - second_half * sine_part,
            second_half * cosine + first_half * sine_part,
        ],
        axis=-1,
    )


def norm_apply(values, gain):
    inverse = lax.rsqrt(jnp.mean(values * values, axis=-1, keepdims=True) + eps)
    return (values * inverse * gain, inverse)


def norm_back(values, inverse, gain, upstream):
    scaled = gain * upstream
    gain_grad = jnp.sum(values * inverse * upstream, axis=0)
    input_grad = inverse * scaled - values * inverse**3 * jnp.mean(
        values * scaled, axis=-1, keepdims=True
    )
    return (input_grad, gain_grad)


def outer_sum(left, right):
    return lax.dot_general(
        left, right, (((0,), (0,)), ((), ())), preferred_element_type=jnp.float32
    )


def times_transposed(left, right):
    return lax.dot_general(
        left, right, (((1,), (1,)), ((), ())), preferred_element_type=jnp.float32
    )


def column_term(left, right):
    return outer_sum(left, right)


def reduce_rows(partial_sum):
    low = partial_sum.astype(jnp.bfloat16)
    pairs, seats = lax.axis_size("gx"), lax.axis_size("seq")
    block = low.shape[0] // (pairs * 2 * seats)
    split = low.reshape(pairs, 2, seats * block, low.shape[1])
    mine = lax.axis_index("core")
    here = lax.dynamic_index_in_dim(split, mine, 1, keepdims=False)
    away = lax.dynamic_index_in_dim(split, 1 - mine, 1, keepdims=False)
    other = lax.ppermute(away, "core", [(0, 1), (1, 0)])
    both = (here.astype(jnp.float32) + other.astype(jnp.float32)).astype(jnp.bfloat16)
    return lax.psum_scatter(
        both.reshape(pairs * seats * block, low.shape[1]),
        ("gx", "seq"),
        scatter_dimension=0,
        tiled=True,
    ).astype(jnp.float32)


def expand_factors(keys_a, keys_b):
    groups_here, keys_here = (keys_a.shape[0], keys_a.shape[1])
    half_a = keys_a.shape[2] // 2
    half_b = keys_b.shape[2] // 2
    key_head = keys_a[..., :half_a].astype(jnp.float32).reshape(groups_here, keys_here, RK, H)
    value_head = keys_a[..., half_a:].astype(jnp.float32).reshape(groups_here, keys_here, RK, H)
    key_dim = keys_b[..., :half_b].astype(jnp.float32).reshape(groups_here, keys_here, RK, HD)
    value_dim = keys_b[..., half_b:].astype(jnp.float32).reshape(groups_here, keys_here, RK, HD)
    return (key_head, key_dim, value_head, value_dim)


def finish_factors(grad_a, grad_b, positions_flat):
    groups_here, rows_count = (grad_a.shape[0], grad_a.shape[1])
    dim_part = rotate(
        grad_b[..., : RK * HD].reshape(groups_here * rows_count, RK, HD), positions_flat, -1.0
    ).reshape(groups_here, rows_count, RK * HD)
    low_b = jnp.concatenate([dim_part, grad_b[..., RK * HD :]], axis=-1).astype(jnp.bfloat16)
    return (grad_a.astype(jnp.bfloat16), low_b)


def shards(
    tokens,
    offsets,
    query_head_weight,
    query_dim_weight,
    key_head_weight,
    key_dim_weight,
    value_head_weight,
    value_dim_weight,
    out_weight,
    attention_gain,
    gate_weight,
    up_weight,
    down_weight,
    feedforward_gain,
    cotangent,
):
    every = ("gx", "core", "seq")
    packed = jnp.concatenate(
        [
            out_weight,
            query_head_weight,
            query_dim_weight,
            key_head_weight,
            key_dim_weight,
            value_head_weight,
            value_dim_weight,
            attention_gain[:, None],
        ],
        axis=1,
    )
    packed_full = lax.all_gather(packed, every, axis=0, tiled=True)
    out_full = packed_full[:, :D]
    joined = packed_full[:, D:-1]
    attention_gain_full = packed_full[:, -1]
    gate_up_full = lax.all_gather(
        jnp.concatenate([gate_weight, up_weight, feedforward_gain[:, None]], axis=1),
        every,
        axis=0,
        tiled=True,
    )
    down_full = lax.all_gather(down_weight, every, axis=0, tiled=True)
    hidden_width = gate_weight.shape[1]
    feedforward_gain_full = gate_up_full[:, -1]
    column_widths = [RQ * H, RQ * HD, RK * H, RK * HD, RK * H, RK * HD]
    cuts = [sum(column_widths[: index + 1]) for index in range(5)]
    scale = HD ** (-0.5)
    groups_here, rows_here = (tokens.shape[0], tokens.shape[1])
    row_count = groups_here * rows_here
    start_row = lax.axis_index("seq") * rows_here
    places = start_row + jnp.arange(rows_here, dtype=jnp.int32)
    in_continuation = places >= PROMPT
    branch_index = jnp.where(in_continuation, (places - PROMPT) // CONT, -1)
    pick_table = (branch_index[:, None] == jnp.arange(NCONT, dtype=jnp.int32)[None, :]).astype(
        jnp.int32
    )
    branch_start = jnp.sum(offsets[:, None, :] * pick_table[None, :, :], axis=-1)
    positions = jnp.where(
        in_continuation[None, :],
        branch_start + ((places - PROMPT) % CONT)[None, :],
        places[None, :],
    ).reshape(row_count)
    prompt_place = jnp.arange(PROMPT, dtype=jnp.int32)
    prompt_allowed = jnp.where(
        in_continuation[None, :, None],
        prompt_place[None, None, :] < branch_start[:, :, None],
        prompt_place[None, None, :] <= places[None, :, None],
    )
    local_allowed = (
        in_continuation[:, None]
        & (branch_index[:, None] == branch_index[None, :])
        & (places[None, :] <= places[:, None])
    )
    allowed = jnp.concatenate(
        [
            prompt_allowed,
            jnp.broadcast_to(local_allowed[None], (groups_here, rows_here, rows_here)),
        ],
        axis=-1,
    )
    flat = tokens.reshape(row_count, D).astype(jnp.float32)
    normed, inverse_first = norm_apply(flat, attention_gain_full.astype(jnp.float32))
    normed_low = normed.astype(jnp.bfloat16)
    projected = jnp.dot(normed_low, joined, preferred_element_type=jnp.float32)
    pieces = jnp.split(projected, cuts, axis=1)
    a_query = pieces[0].reshape(row_count, RQ, H)
    b_query = rotate(pieces[1].reshape(row_count, RQ, HD), positions, 1.0)
    b_key = rotate(pieces[3].reshape(row_count, RK, HD), positions, 1.0).reshape(row_count, RK * HD)
    factor_a = (
        jnp.concatenate([pieces[2], pieces[4]], axis=1)
        .astype(jnp.bfloat16)
        .reshape(groups_here, rows_here, 2 * RK * H)
    )
    factor_b = (
        jnp.concatenate([b_key, pieces[5]], axis=1)
        .astype(jnp.bfloat16)
        .reshape(groups_here, rows_here, 2 * RK * HD)
    )
    query = (
        (jnp.einsum("nrh,nrd->nhd", a_query, b_query) / RQ)
        .astype(jnp.bfloat16)
        .reshape(groups_here, rows_here, H, HD)
    )
    every_a, every_b = (
        lax.all_gather(factor_a, "seq", axis=1, tiled=True),
        lax.all_gather(factor_b, "seq", axis=1, tiled=True),
    )
    keys_a = jnp.concatenate([every_a[:, :PROMPT], factor_a], axis=1)
    keys_b = jnp.concatenate([every_b[:, :PROMPT], factor_b], axis=1)
    key_head, key_dim, value_head, value_dim = expand_factors(keys_a, keys_b)
    keys = (jnp.einsum("gkrh,gkrd->gkhd", key_head, key_dim) / RK).astype(jnp.bfloat16)
    values = (jnp.einsum("gkrh,gkrd->gkhd", value_head, value_dim) / RK).astype(jnp.bfloat16)

    def attend(inputs):
        query_group, keys_group, values_group, allowed_group = inputs
        scores = (
            jnp.einsum("qhd,khd->hqk", query_group, keys_group, preferred_element_type=jnp.float32)
            * scale
        )
        scores = jnp.where(allowed_group[None], scores, masked_score)
        top_score = jnp.max(scores, axis=-1, keepdims=True)
        exponential = jnp.exp(scores - top_score)
        row_total = jnp.sum(exponential, axis=-1, keepdims=True)
        probabilities = (exponential / row_total).astype(jnp.bfloat16)
        mixed_group = jnp.einsum(
            "hqk,khd->qhd", probabilities, values_group, preferred_element_type=jnp.float32
        ).astype(jnp.bfloat16)
        return (mixed_group, top_score + jnp.log(row_total))

    mixed, log_total = lax.map(attend, (query, keys, values, allowed))
    mixed_flat = mixed.reshape(row_count, H * HD)
    middle = flat + jnp.dot(mixed_flat, out_full, preferred_element_type=jnp.float32)
    normed_second, inverse_second = norm_apply(middle, feedforward_gain_full.astype(jnp.float32))
    second_low = normed_second.astype(jnp.bfloat16)
    gate_full = gate_up_full[:, :hidden_width]
    up_full = gate_up_full[:, hidden_width : 2 * hidden_width]
    gate = jnp.dot(second_low, gate_full, preferred_element_type=jnp.float32)
    upper = jnp.dot(second_low, up_full, preferred_element_type=jnp.float32)
    gate_sigmoid = jax.nn.sigmoid(gate)
    swish = gate * gate_sigmoid
    hidden = (swish * upper).astype(jnp.bfloat16)
    result = middle + jnp.dot(hidden, down_full, preferred_element_type=jnp.float32)
    output = result.astype(jnp.bfloat16).reshape(groups_here, rows_here, D)
    upstream = cotangent.reshape(row_count, D).astype(jnp.float32)
    upstream_low = upstream.astype(jnp.bfloat16)
    down_out = reduce_rows(column_term(hidden, upstream_low))
    hidden_grad = times_transposed(upstream_low, down_full)
    up_rows = (hidden_grad * swish).astype(jnp.bfloat16)
    gate_rows = (hidden_grad * upper * gate_sigmoid * (1.0 + gate * (1.0 - gate_sigmoid))).astype(
        jnp.bfloat16
    )
    gate_up_rows = jnp.concatenate([gate_rows, up_rows], axis=1)
    gate_up_out = reduce_rows(column_term(second_low, gate_up_rows))
    gate_out = gate_up_out[:, :hidden_width]
    up_out = gate_up_out[:, hidden_width:]
    second_grad = times_transposed(gate_rows, gate_full) + times_transposed(up_rows, up_full)
    middle_part, feedforward_gain_grad = norm_back(
        middle, inverse_second, feedforward_gain_full.astype(jnp.float32), second_grad
    )
    middle_grad = upstream + middle_part
    branch_low = middle_grad.astype(jnp.bfloat16)
    out_weight_out = reduce_rows(column_term(mixed_flat, branch_low))
    mixed_grad = (
        times_transposed(branch_low, out_full)
        .astype(jnp.bfloat16)
        .reshape(groups_here, rows_here, H, HD)
    )

    def attend_back(inputs):
        query_group, keys_group, values_group, allowed_group, log_group, mixed_grad_group = inputs
        scores = (
            jnp.einsum("qhd,khd->hqk", query_group, keys_group, preferred_element_type=jnp.float32)
            * scale
        )
        scores = jnp.where(allowed_group[None], scores, masked_score)
        probabilities = jnp.exp(scores - log_group)
        prob_low = probabilities.astype(jnp.bfloat16)
        prob_grad = jnp.einsum(
            "qhd,khd->hqk", mixed_grad_group, values_group, preferred_element_type=jnp.float32
        )
        values_grad = jnp.einsum(
            "hqk,qhd->khd", prob_low, mixed_grad_group, preferred_element_type=jnp.float32
        )
        row_inner = jnp.sum(prob_grad * probabilities, axis=-1, keepdims=True)
        score_grad = (probabilities * (prob_grad - row_inner) * scale).astype(jnp.bfloat16)
        query_grad = jnp.einsum(
            "hqk,khd->qhd", score_grad, keys_group, preferred_element_type=jnp.float32
        )
        keys_grad = jnp.einsum(
            "hqk,qhd->khd", score_grad, query_group, preferred_element_type=jnp.float32
        )
        return (query_grad, keys_grad, values_grad)

    query_grad, keys_grad, values_grad = lax.map(
        attend_back, (query, keys, values, allowed, log_total, mixed_grad)
    )
    query_grad = query_grad.reshape(row_count, H, HD)
    a_query_grad = jnp.einsum("nhd,nrd->nrh", query_grad, b_query) / RQ
    b_query_grad = rotate(jnp.einsum("nhd,nrh->nrd", query_grad, a_query) / RQ, positions, -1.0)
    keys_here = keys_grad.shape[1]
    key_head_grad = jnp.einsum("gkhd,gkrd->gkrh", keys_grad, key_dim) / RK
    key_dim_grad = jnp.einsum("gkhd,gkrh->gkrd", keys_grad, key_head) / RK
    value_head_grad = jnp.einsum("gkhd,gkrd->gkrh", values_grad, value_dim) / RK
    value_dim_grad = jnp.einsum("gkhd,gkrh->gkrd", values_grad, value_head) / RK
    grad_a = jnp.concatenate(
        [
            key_head_grad.reshape(groups_here, keys_here, RK * H),
            value_head_grad.reshape(groups_here, keys_here, RK * H),
        ],
        axis=-1,
    )
    grad_b = jnp.concatenate(
        [
            key_dim_grad.reshape(groups_here, keys_here, RK * HD),
            value_dim_grad.reshape(groups_here, keys_here, RK * HD),
        ],
        axis=-1,
    )

    def place_rows(grad_part):
        column_count = grad_part.shape[2]
        spread = jnp.concatenate(
            [
                grad_part[:, :PROMPT],
                jnp.zeros((groups_here, SEQLEN - PROMPT, column_count), jnp.float32),
            ],
            axis=1,
        )
        current = lax.dynamic_slice_in_dim(spread, start_row, rows_here, 1)
        return lax.dynamic_update_slice_in_dim(
            spread, current + grad_part[:, PROMPT:], start_row, 1
        )

    summed_a, summed_b = (
        lax.psum_scatter(
            place_rows(grad_a).astype(jnp.bfloat16), "seq", scatter_dimension=1, tiled=True
        ).astype(jnp.float32),
        lax.psum_scatter(
            place_rows(grad_b).astype(jnp.bfloat16), "seq", scatter_dimension=1, tiled=True
        ).astype(jnp.float32),
    )
    owned_a, owned_b = finish_factors(summed_a, summed_b, positions)
    owned_a = owned_a.reshape(row_count, 2 * RK * H)
    owned_b = owned_b.reshape(row_count, 2 * RK * HD)
    factor_grad = jnp.concatenate(
        [
            a_query_grad.reshape(row_count, RQ * H).astype(jnp.bfloat16),
            b_query_grad.reshape(row_count, RQ * HD).astype(jnp.bfloat16),
            owned_a[:, : RK * H],
            owned_b[:, : RK * HD],
            owned_a[:, RK * H :],
            owned_b[:, RK * HD :],
        ],
        axis=1,
    )
    first_grad = times_transposed(factor_grad, joined)
    input_part, attention_gain_grad = norm_back(
        flat, inverse_first, attention_gain_full.astype(jnp.float32), first_grad
    )
    input_gradient = (
        (middle_grad + input_part).astype(jnp.bfloat16).reshape(groups_here, rows_here, D)
    )
    joined_out = reduce_rows(
        jnp.concatenate(
            [
                column_term(normed_low, factor_grad),
                attention_gain_grad[:, None],
                feedforward_gain_grad[:, None],
            ],
            axis=1,
        )
    )
    grad_pieces = jnp.split(joined_out[:, :-2], cuts, axis=1)
    attention_gain_out = joined_out[:, -2]
    feedforward_gain_out = joined_out[:, -1]
    return (
        output,
        input_gradient,
        grad_pieces[0],
        grad_pieces[1],
        grad_pieces[2],
        grad_pieces[3],
        grad_pieces[4],
        grad_pieces[5],
        out_weight_out,
        attention_gain_out,
        gate_out,
        up_out,
        down_out,
        feedforward_gain_out,
    )


def solution(mesh):
    groups, seats = mesh.shape["grp"], mesh.shape["seq"]
    fine = jax.sharding.Mesh(
        mesh.devices.reshape(groups // 2, 2, seats), ("gx", "core", "seq")
    )
    grp = ("gx", "core")
    rows = ("gx", "core", "seq")
    token = P(grp, "seq", None)
    weight = P(rows, None)
    gain = P(rows)
    placed = (token, P(grp, None)) + (weight,) * 7 + (gain,) + (weight,) * 3 + (gain, token)
    return jax.shard_map(
        shards,
        mesh=fine,
        in_specs=placed,
        out_specs=(token, token) + (weight,) * 7 + (gain,) + (weight,) * 3 + (gain,),
        check_vma=False,
    )
```

```python
import jax
import jax.numpy as jnp
from jax import lax
from jax.experimental import pallas as pl
from jax.experimental.pallas import tpu as pltpu
from jax.sharding import PartitionSpec as P

D = 1024
H = 16
HD = 64
RQ = 6
RK = 2
PROMPT = 1024
CONT = 128
NCONT = 8


eps = 1e-06
masked_score = -1e30


def norm_apply(values, gain):
    inverse = lax.rsqrt(jnp.mean(values * values, axis=-1, keepdims=True) + eps)
    return (values * inverse * gain, inverse)


def norm_back(values, inverse, gain, upstream):
    scaled = gain * upstream
    gain_grad = jnp.sum(values * inverse * upstream, axis=0)
    input_grad = inverse * scaled - values * inverse**3 * jnp.mean(
        values * scaled, axis=-1, keepdims=True
    )
    return (input_grad, gain_grad)


def outer_sum(left, right):
    return lax.dot_general(
        left, right, (((0,), (0,)), ((), ())), preferred_element_type=jnp.float32
    )


def times_transposed(left, right):
    return lax.dot_general(
        left, right, (((1,), (1,)), ((), ())), preferred_element_type=jnp.float32
    )


def reduce_rows(partial_sum):
    low = partial_sum.astype(jnp.bfloat16)
    pairs, seats = lax.axis_size("gx"), lax.axis_size("seq")
    block = low.shape[0] // (pairs * 2 * seats)
    split = low.reshape(pairs, 2, seats * block, low.shape[1])
    mine = lax.axis_index("core")
    here = lax.dynamic_index_in_dim(split, mine, 1, keepdims=False)
    away = lax.dynamic_index_in_dim(split, 1 - mine, 1, keepdims=False)
    other = lax.ppermute(away, "core", [(0, 1), (1, 0)])
    both = (here.astype(jnp.float32) + other.astype(jnp.float32)).astype(jnp.bfloat16)
    return lax.psum_scatter(
        both.reshape(pairs * seats * block, low.shape[1]),
        ("gx", "seq"),
        scatter_dimension=0,
        tiled=True,
    ).astype(jnp.float32)


def rank_rows(head_ref, dim_ref, lead, head_base, dim_base, ranks, head):
    total = None
    for r in range(ranks):
        row = head_ref[lead + (pl.ds(head_base + r * H + head, 1), slice(None))]
        dims = dim_ref[lead + (slice(dim_base + r * HD, dim_base + (r + 1) * HD), slice(None))]
        term = row * dims
        total = term if total is None else total + term
    return total


def head_pair(head_ref, dim_ref, lead, head_base, dim_base, ranks, pair):
    both = [
        rank_rows(head_ref, dim_ref, lead, head_base, dim_base, ranks, 2 * pair + j)
        * (1.0 / ranks)
        for j in range(2)
    ]
    return jnp.concatenate(both, axis=0)


def stage_factors(every_ref, local_ref, heads, dims):
    chunks = heads.shape[0]
    for c in range(chunks):
        block = local_ref[0] if c == chunks - 1 else every_ref[c, 0]
        dims[c] = block[: 4 * HD].astype(jnp.float32)
        heads[c] = block[4 * HD :].astype(jnp.float32)


def stage_bias(branch_ref, limit_ref, bias):
    chunks, rows = bias.shape[0], bias.shape[1]
    limit = limit_ref[0]
    key = lax.broadcasted_iota(jnp.int32, (rows, rows), 1)
    row = lax.broadcasted_iota(jnp.int32, (rows, rows), 0)
    for c in range(chunks - 1):
        bias[c] = jnp.where(key + c * rows < limit, 0.0, masked_score)
    local = (key <= row) & (key // CONT == row // CONT) & (branch_ref[0] > 0)
    bias[chunks - 1] = jnp.where(local, 0.0, masked_score)


def lane_split(pair_block):
    lane = lax.broadcasted_iota(jnp.int32, pair_block.shape, 1)
    first = jnp.where(lane < HD, pair_block, 0.0)
    second = jnp.where(lane < HD, 0.0, pair_block)
    return jnp.concatenate([first, second], axis=0)


def lane_join(stacked):
    rows = stacked.shape[0] // 2
    lane = lax.broadcasted_iota(jnp.int32, (rows, stacked.shape[1]), 1)
    return jnp.where(lane < HD, stacked[:rows], stacked[rows:])


def diagonal_pair(pair_t):
    row = lax.broadcasted_iota(jnp.int32, pair_t.shape, 0)
    first = jnp.where(row < HD, pair_t, 0.0)
    second = jnp.where(row < HD, 0.0, pair_t)
    return jnp.concatenate([first, second], axis=1)


def dot_nn(left, right):
    return lax.dot_general(
        left, right, (((1,), (0,)), ((), ())), preferred_element_type=jnp.float32
    )


def dot_nt(left, right):
    return lax.dot_general(
        left, right, (((1,), (1,)), ((), ())), preferred_element_type=jnp.float32
    )


def attend_kernel(
    branch_ref, limit_ref, qh_ref, qd_ref, every_ref, local_ref, mixed_ref, log_ref, heads, dims, bias
):
    pair = pl.program_id(1)
    chunks, rows = bias.shape[0], bias.shape[1]

    @pl.when(pair == 0)
    def _():
        stage_factors(every_ref, local_ref, heads, dims)
        stage_bias(branch_ref, limit_ref, bias)
        log_ref[...] = jnp.zeros_like(log_ref)

    query_t = head_pair(qh_ref, qd_ref, (), 0, 0, RQ, pair)
    query = query_t.T.astype(jnp.bfloat16).astype(jnp.float32) * HD ** (-0.5)
    query = lane_split(query).astype(jnp.bfloat16)
    scores = []
    top = None
    for c in range(chunks):
        key_t = head_pair(heads, dims, (c,), 0, 0, RK, pair).astype(jnp.bfloat16)
        score = dot_nn(query, key_t)
        score = score + jnp.concatenate([bias[c], bias[c]], axis=0)
        scores.append(score)
        top = score if top is None else jnp.maximum(top, score)
    top = jnp.max(top, axis=-1, keepdims=True)
    total = None
    mixed = None
    for c in range(chunks):
        value_t = head_pair(heads, dims, (c,), RK * H, RK * HD, RK, pair).astype(jnp.bfloat16)
        weight = jnp.exp(scores[c] - top)
        total = weight if total is None else total + weight
        part = dot_nt(weight.astype(jnp.bfloat16), value_t)
        mixed = part if mixed is None else mixed + part
    total = jnp.sum(total, axis=-1, keepdims=True)
    mixed_ref[0] = lane_join(mixed / total).astype(jnp.bfloat16)
    log_total = top + jnp.log(total)
    lane = lax.broadcasted_iota(jnp.int32, (rows, 128), 1)
    kept = log_ref[0]
    for j in range(2):
        kept = jnp.where(lane == 2 * pair + j, log_total[j * rows : (j + 1) * rows], kept)
    log_ref[0] = kept


def attend_back_kernel(
    branch_ref, limit_ref, qh_ref, qd_ref, every_ref, local_ref, mixed_ref, upstream_ref, log_ref,
    qh_out, qd_out, factor_out, heads, dims, bias, heads_sum, dims_sum,
):
    pair = pl.program_id(1)
    chunks, rows = bias.shape[0], bias.shape[1]

    @pl.when(pair == 0)
    def _():
        stage_factors(every_ref, local_ref, heads, dims)
        stage_bias(branch_ref, limit_ref, bias)
        dims_sum[...] = jnp.zeros_like(dims_sum)
        qd_out[...] = jnp.zeros_like(qd_out)

    query_t = head_pair(qh_ref, qd_ref, (), 0, 0, RQ, pair)
    query_t = query_t.astype(jnp.bfloat16).astype(jnp.float32) * HD ** (-0.5)
    query = lane_split(query_t.T).astype(jnp.bfloat16)
    query_t = diagonal_pair(query_t).astype(jnp.bfloat16)
    upstream = upstream_ref[0].astype(jnp.float32)
    inner = lane_split(upstream * mixed_ref[0].astype(jnp.float32))
    inner = jnp.sum(inner, axis=-1, keepdims=True)
    upstream_t = diagonal_pair(upstream.T).astype(jnp.bfloat16)
    upstream = lane_split(upstream).astype(jnp.bfloat16)
    lane = lax.broadcasted_iota(jnp.int32, (rows, 128), 1)
    log_total = jnp.concatenate(
        [
            jnp.sum(jnp.where(lane == 2 * pair + j, log_ref[0], 0.0), axis=-1, keepdims=True)
            for j in range(2)
        ],
        axis=0,
    )
    query_grad = None
    for c in range(chunks):
        key_t = head_pair(heads, dims, (c,), 0, 0, RK, pair).astype(jnp.bfloat16)
        value_t = head_pair(heads, dims, (c,), RK * H, RK * HD, RK, pair).astype(jnp.bfloat16)
        score = dot_nn(query, key_t)
        score = score + jnp.concatenate([bias[c], bias[c]], axis=0)
        weight = jnp.exp(score - log_total)
        weight_grad = dot_nn(upstream, value_t)
        score_grad = (weight * (weight_grad - inner)).astype(jnp.bfloat16)
        part = dot_nt(score_grad, key_t)
        query_grad = part if query_grad is None else query_grad + part
        key_grad = dot_nn(query_t, score_grad)
        value_grad = dot_nn(upstream_t, weight.astype(jnp.bfloat16))
        for kind, grad in ((0, key_grad), (1, value_grad)):
            for j in range(2):
                half = grad[j * HD : (j + 1) * HD] * (1.0 / RK)
                for r in range(RK):
                    place = kind * RK * H + r * H + 2 * pair + j
                    base = kind * RK * HD + r * HD
                    row = heads[c, pl.ds(place, 1), :]
                    block = dims[c, base : base + HD, :]
                    heads_sum[c, pl.ds(place, 1), :] = jnp.sum(half * block, axis=0, keepdims=True)
                    dims_sum[c, base : base + HD, :] += half * row
    query_grad = (lane_join(query_grad) * (HD ** (-0.5) / RQ)).T
    for j in range(2):
        half = query_grad[j * HD : (j + 1) * HD]
        for r in range(RQ):
            place = r * H + 2 * pair + j
            row = qh_ref[pl.ds(place, 1), :]
            block = qd_ref[r * HD : (r + 1) * HD, :]
            qh_out[pl.ds(place, 1), :] = jnp.sum(half * block, axis=0, keepdims=True)
            qd_out[r * HD : (r + 1) * HD, :] += half * row

    @pl.when(pair == H // 2 - 1)
    def _():
        for c in range(chunks):
            factor_out[c, 0, : 4 * HD] = dims_sum[c].astype(jnp.bfloat16)
            factor_out[c, 0, 4 * HD :] = heads_sum[c].astype(jnp.bfloat16)


def attention_specs(rows, chunks):
    width = 4 * HD + 4 * H
    return [
        pl.BlockSpec((1, rows, 1), lambda g, p, *_: (g, 0, 0)),
        pl.BlockSpec((RQ * H, rows), lambda g, p, *_: (0, g)),
        pl.BlockSpec((RQ * HD, rows), lambda g, p, *_: (0, g)),
        pl.BlockSpec((chunks - 1, 1, width, rows), lambda g, p, *_: (0, g, 0, 0)),
        pl.BlockSpec((1, width, rows), lambda g, p, *_: (g, 0, 0)),
    ]


def attention_scratch(rows, chunks):
    return [
        pltpu.VMEM((chunks, 4 * H, rows), jnp.float32),
        pltpu.VMEM((chunks, 4 * HD, rows), jnp.float32),
        pltpu.VMEM((chunks, rows, rows), jnp.float32),
    ]


def attend(branch, limit, qh, qd, every, local):
    groups_here, width, rows = local.shape
    chunks = PROMPT // rows + 1
    pair_block = pl.BlockSpec((1, rows, 2 * HD), lambda g, p, *_: (g, 0, p))
    work = groups_here * H * rows * rows * chunks
    return pl.pallas_call(
        attend_kernel,
        grid_spec=pltpu.PrefetchScalarGridSpec(
            num_scalar_prefetch=1,
            grid=(groups_here, H // 2),
            in_specs=attention_specs(rows, chunks),
            out_specs=[
                pair_block,
                pl.BlockSpec((1, rows, 128), lambda g, p, *_: (g, 0, 0)),
            ],
            scratch_shapes=attention_scratch(rows, chunks),
        ),
        out_shape=[
            jax.ShapeDtypeStruct((groups_here, rows, H * HD), jnp.bfloat16),
            jax.ShapeDtypeStruct((groups_here, rows, 128), jnp.float32),
        ],
        cost_estimate=pl.CostEstimate(
            flops=work * HD * 8, transcendentals=work, bytes_accessed=8 * 2**20
        ),
        compiler_params=pltpu.CompilerParams(vmem_limit_bytes=56 * 2**20),
        name="attend",
    )(branch, limit, qh, qd, every, local)


def attend_back(branch, limit, qh, qd, every, local, mixed, upstream, log_total):
    groups_here, width, rows = local.shape
    chunks = PROMPT // rows + 1
    pair_block = pl.BlockSpec((1, rows, 2 * HD), lambda g, p, *_: (g, 0, p))
    work = groups_here * H * rows * rows * chunks
    return pl.pallas_call(
        attend_back_kernel,
        grid_spec=pltpu.PrefetchScalarGridSpec(
            num_scalar_prefetch=1,
            grid=(groups_here, H // 2),
            in_specs=attention_specs(rows, chunks)
            + [
                pair_block,
                pair_block,
                pl.BlockSpec((1, rows, 128), lambda g, p, *_: (g, 0, 0)),
            ],
            out_specs=[
                pl.BlockSpec((RQ * H, rows), lambda g, p, *_: (0, g)),
                pl.BlockSpec((RQ * HD, rows), lambda g, p, *_: (0, g)),
                pl.BlockSpec((chunks, 1, width, rows), lambda g, p, *_: (0, g, 0, 0)),
            ],
            scratch_shapes=attention_scratch(rows, chunks)
            + [
                pltpu.VMEM((chunks, 4 * H, rows), jnp.float32),
                pltpu.VMEM((chunks, 4 * HD, rows), jnp.float32),
            ],
        ),
        out_shape=[
            jax.ShapeDtypeStruct(qh.shape, jnp.float32),
            jax.ShapeDtypeStruct(qd.shape, jnp.float32),
            jax.ShapeDtypeStruct((chunks, groups_here, width, rows), jnp.bfloat16),
        ],
        cost_estimate=pl.CostEstimate(
            flops=work * HD * 20, transcendentals=work, bytes_accessed=16 * 2**20
        ),
        compiler_params=pltpu.CompilerParams(vmem_limit_bytes=60 * 2**20),
        name="attend_back",
    )(branch, limit, qh, qd, every, local, mixed, upstream, log_total)


def rotate_rows(values, ranks, cosine, sine_part):
    turned = []
    half = HD // 2
    for r in range(ranks):
        first = values[r * HD : r * HD + half]
        second = values[r * HD + half : (r + 1) * HD]
        turned.append(first * cosine - second * sine_part)
        turned.append(second * cosine + first * sine_part)
    return jnp.concatenate(turned, axis=0)


def shards(
    tokens,
    offsets,
    query_head_weight,
    query_dim_weight,
    key_head_weight,
    key_dim_weight,
    value_head_weight,
    value_dim_weight,
    out_weight,
    attention_gain,
    gate_weight,
    up_weight,
    down_weight,
    feedforward_gain,
    cotangent,
):
    every = ("gx", "core", "seq")
    packed = jnp.concatenate(
        [
            out_weight,
            key_dim_weight,
            value_dim_weight,
            key_head_weight,
            value_head_weight,
            query_dim_weight,
            query_head_weight,
            attention_gain[:, None],
        ],
        axis=1,
    )
    packed_full = lax.all_gather(packed, every, axis=0, tiled=True)
    out_full = packed_full[:, :D]
    joined = packed_full[:, D:-1]
    attention_gain_full = packed_full[:, -1]
    gate_up_full = lax.all_gather(
        jnp.concatenate([gate_weight, up_weight, feedforward_gain[:, None]], axis=1),
        every,
        axis=0,
        tiled=True,
    )
    down_full = lax.all_gather(down_weight, every, axis=0, tiled=True)
    hidden_width = gate_weight.shape[1]
    feedforward_gain_full = gate_up_full[:, -1]
    factor_width = 2 * RK * (HD + H)
    groups_here, rows_here = (tokens.shape[0], tokens.shape[1])
    row_count = groups_here * rows_here
    seat = lax.axis_index("seq")
    start_row = seat * rows_here
    places = start_row + jnp.arange(rows_here, dtype=jnp.int32)
    in_continuation = places >= PROMPT
    branch_index = jnp.where(in_continuation, (places - PROMPT) // CONT, -1)
    pick_table = (branch_index[:, None] == jnp.arange(NCONT, dtype=jnp.int32)[None, :]).astype(
        jnp.int32
    )
    branch_start = jnp.sum(offsets[:, None, :] * pick_table[None, :, :], axis=-1)
    positions = jnp.where(
        in_continuation[None, :],
        branch_start + ((places - PROMPT) % CONT)[None, :],
        places[None, :],
    ).reshape(row_count)
    limit = jnp.where(in_continuation[None, :], branch_start, places[None, :] + 1)[:, :, None]
    branch = (start_row >= PROMPT).astype(jnp.int32).reshape(1)
    frequency = 10000.0 ** (-2.0 * jnp.arange(HD // 2, dtype=jnp.float32) / HD)
    angles = frequency[:, None] * positions.astype(jnp.float32)[None, :]
    cosine, sine = jnp.cos(angles), jnp.sin(angles)

    flat = tokens.reshape(row_count, D).astype(jnp.float32)
    normed, inverse_first = norm_apply(flat, attention_gain_full.astype(jnp.float32))
    normed_low = normed.astype(jnp.bfloat16)
    projected = lax.dot_general(
        joined, normed_low, (((0,), (1,)), ((), ())), preferred_element_type=jnp.float32
    )
    local = jnp.concatenate(
        [
            rotate_rows(projected[: RK * HD], RK, cosine, sine),
            projected[RK * HD : factor_width],
        ],
        axis=0,
    ).astype(jnp.bfloat16)
    local = local.reshape(factor_width, groups_here, rows_here).transpose(1, 0, 2)
    every_factor = lax.all_gather(local, "seq", axis=0, tiled=False)
    query_dim = rotate_rows(projected[factor_width : factor_width + RQ * HD], RQ, cosine, sine)
    query_head = projected[factor_width + RQ * HD :]
    mixed, log_total = attend(branch, limit, query_head, query_dim, every_factor, local)
    mixed_flat = mixed.reshape(row_count, H * HD)
    middle = flat + jnp.dot(mixed_flat, out_full, preferred_element_type=jnp.float32)
    normed_second, inverse_second = norm_apply(middle, feedforward_gain_full.astype(jnp.float32))
    second_low = normed_second.astype(jnp.bfloat16)
    gate_full = gate_up_full[:, :hidden_width]
    up_full = gate_up_full[:, hidden_width : 2 * hidden_width]
    gate = jnp.dot(second_low, gate_full, preferred_element_type=jnp.float32)
    upper = jnp.dot(second_low, up_full, preferred_element_type=jnp.float32)
    gate_sigmoid = jax.nn.sigmoid(gate)
    swish = gate * gate_sigmoid
    hidden = (swish * upper).astype(jnp.bfloat16)
    result = middle + jnp.dot(hidden, down_full, preferred_element_type=jnp.float32)
    output = result.astype(jnp.bfloat16).reshape(groups_here, rows_here, D)
    upstream = cotangent.reshape(row_count, D).astype(jnp.float32)
    upstream_low = upstream.astype(jnp.bfloat16)
    down_out = reduce_rows(outer_sum(hidden, upstream_low))
    hidden_grad = times_transposed(upstream_low, down_full)
    up_rows = (hidden_grad * swish).astype(jnp.bfloat16)
    gate_rows = (hidden_grad * upper * gate_sigmoid * (1.0 + gate * (1.0 - gate_sigmoid))).astype(
        jnp.bfloat16
    )
    gate_up_rows = jnp.concatenate([gate_rows, up_rows], axis=1)
    gate_up_out = reduce_rows(outer_sum(second_low, gate_up_rows))
    gate_out = gate_up_out[:, :hidden_width]
    up_out = gate_up_out[:, hidden_width:]
    second_grad = times_transposed(gate_rows, gate_full) + times_transposed(up_rows, up_full)
    middle_part, feedforward_gain_grad = norm_back(
        middle, inverse_second, feedforward_gain_full.astype(jnp.float32), second_grad
    )
    middle_grad = upstream + middle_part
    branch_low = middle_grad.astype(jnp.bfloat16)
    out_weight_out = reduce_rows(outer_sum(mixed_flat, branch_low))
    mixed_grad = (
        times_transposed(branch_low, out_full)
        .astype(jnp.bfloat16)
        .reshape(groups_here, rows_here, H * HD)
    )
    query_head_grad, query_dim_grad, factor_part = attend_back(
        branch, limit, query_head, query_dim, every_factor, local, mixed, mixed_grad, log_total
    )
    seats = lax.axis_size("seq")
    prompt_seats = PROMPT // rows_here
    own = (jnp.arange(seats) == seat)[:, None, None, None]
    spread = jnp.concatenate(
        [
            factor_part[:prompt_seats],
            jnp.where(own[prompt_seats:], factor_part[prompt_seats:], jnp.zeros((), jnp.bfloat16)),
        ],
        axis=0,
    )
    summed = lax.psum_scatter(spread, "seq", scatter_dimension=0, tiled=False)
    summed = summed.astype(jnp.float32).transpose(1, 0, 2).reshape(factor_width, row_count)
    factor_grad = jnp.concatenate(
        [
            rotate_rows(summed[: RK * HD], RK, cosine, -sine),
            summed[RK * HD :],
            rotate_rows(query_dim_grad, RQ, cosine, -sine),
            query_head_grad,
        ],
        axis=0,
    ).astype(jnp.bfloat16)
    first_grad = lax.dot_general(
        factor_grad, joined, (((0,), (1,)), ((), ())), preferred_element_type=jnp.float32
    )
    input_part, attention_gain_grad = norm_back(
        flat, inverse_first, attention_gain_full.astype(jnp.float32), first_grad
    )
    input_gradient = (
        (middle_grad + input_part).astype(jnp.bfloat16).reshape(groups_here, rows_here, D)
    )
    joined_grad = lax.dot_general(
        normed_low, factor_grad, (((0,), (1,)), ((), ())), preferred_element_type=jnp.float32
    )
    joined_out = reduce_rows(
        jnp.concatenate(
            [joined_grad, attention_gain_grad[:, None], feedforward_gain_grad[:, None]], axis=1
        )
    )
    widths = [RK * HD, RK * HD, RK * H, RK * H, RQ * HD, RQ * H, 1, 1]
    cuts = [sum(widths[: index + 1]) for index in range(len(widths) - 1)]
    pieces = jnp.split(joined_out, cuts, axis=1)
    return (
        output,
        input_gradient,
        pieces[5],
        pieces[4],
        pieces[2],
        pieces[0],
        pieces[3],
        pieces[1],
        out_weight_out,
        pieces[6][:, 0],
        gate_out,
        up_out,
        down_out,
        pieces[7][:, 0],
    )


def solution(mesh):
    groups, seats = mesh.shape["grp"], mesh.shape["seq"]
    fine = jax.sharding.Mesh(
        mesh.devices.reshape(groups // 2, 2, seats), ("gx", "core", "seq")
    )
    grp = ("gx", "core")
    rows = ("gx", "core", "seq")
    token = P(grp, "seq", None)
    weight = P(rows, None)
    gain = P(rows)
    placed = (token, P(grp, None)) + (weight,) * 7 + (gain,) + (weight,) * 3 + (gain, token)
    return jax.shard_map(
        shards,
        mesh=fine,
        in_specs=placed,
        out_specs=(token, token) + (weight,) * 7 + (gain,) + (weight,) * 3 + (gain,),
        check_vma=False,
    )
```

```python
import jax
import jax.numpy as jnp
from jax import lax
from jax.experimental import pallas as pl
from jax.experimental.pallas import tpu as pltpu
from jax.sharding import PartitionSpec as P


D = 1024
H = 16
HD = 64
RQ = 6
RK = 2
PROMPT = 1024
CONT = 128
NCONT = 8


eps = 1e-06
masked_score = -1e30


def norm_apply(values, gain):
    inverse = lax.rsqrt(jnp.mean(values * values, axis=-1, keepdims=True) + eps)
    return (values * inverse * gain, inverse)


def norm_back(values, inverse, gain, upstream):
    scaled = gain * upstream
    gain_grad = jnp.sum(values * inverse * upstream, axis=0)
    input_grad = inverse * scaled - values * inverse**3 * jnp.mean(
        values * scaled, axis=-1, keepdims=True
    )
    return (input_grad, gain_grad)


def outer_sum(left, right):
    return lax.dot_general(
        left, right, (((0,), (0,)), ((), ())), preferred_element_type=jnp.float32
    )


def times_transposed(left, right):
    return lax.dot_general(
        left, right, (((1,), (1,)), ((), ())), preferred_element_type=jnp.float32
    )


def halve(blocks, axis, dim, tie=None):
    if lax.axis_size(axis) != 2:
        total = lax.psum_scatter(
            blocks.astype(jnp.bfloat16), axis, scatter_dimension=dim, tiled=False
        ).astype(jnp.float32)
        return total if tie is None else (total, tie)
    mine = lax.axis_index(axis)
    keep = lax.dynamic_index_in_dim(blocks, mine, dim, keepdims=False)
    away = lax.dynamic_index_in_dim(blocks, 1 - mine, dim, keepdims=False).astype(jnp.bfloat16)
    if tie is not None:
        away, tie = lax.optimization_barrier((away, tie))
    other = lax.ppermute(away, axis, [(0, 1), (1, 0)])
    total = keep.astype(jnp.float32) + other.astype(jnp.float32)
    return total if tie is None else (total, tie)


def shift_sum(blocks, axis, owners):
    count = lax.axis_size(axis)
    mine = lax.axis_index(axis)
    total = lax.dynamic_index_in_dim(
        blocks, jnp.minimum(mine, owners - 1), 0, keepdims=False
    ).astype(jnp.float32)
    low = blocks.astype(jnp.bfloat16)
    for step in range(1, count):
        target = jnp.minimum((mine + step) % count, owners - 1)
        away = lax.dynamic_index_in_dim(low, target, 0, keepdims=False)
        pairs = [(i, (i + step) % count) for i in range(count) if (i + step) % count < owners]
        total = total + lax.ppermute(away, axis, pairs).astype(jnp.float32)
    return total


def by_seat(rows):
    sizes = [lax.axis_size(axis) for axis in ("gx", "core", "z", "y")]
    return sizes + [rows // (sizes[0] * sizes[1] * sizes[2] * sizes[3])]


def to_seat(summed, x_first):
    return second_step(first_step(summed, x_first), x_first)


def first_step(summed, x_first, tie=None):
    return halve(summed, "gx" if x_first else "y", 0 if x_first else 2, tie)


def second_step(summed, x_first, tie=None):
    return halve(summed, "y" if x_first else "gx", 1 if x_first else 0, tie)


def split_columns(left, part):
    pairs, cores, deep, wide, rows = by_seat(left.shape[1])
    width = deep * wide * rows
    return jnp.concatenate(
        [
            lax.dynamic_slice_in_dim(left, (pair * cores + part) * width, width, 1)
            for pair in range(pairs)
        ],
        axis=1,
    )


def double(blocks, axis, dim):
    if lax.axis_size(axis) != 2:
        return lax.all_gather(blocks, axis, axis=dim, tiled=False)
    other = lax.ppermute(blocks, axis, [(0, 1), (1, 0)])
    return jnp.where(
        lax.axis_index(axis) == 0,
        jnp.stack([blocks, other], axis=dim),
        jnp.stack([other, blocks], axis=dim),
    )


def shift_gather(block, axis):
    count = lax.axis_size(axis)
    mine = lax.axis_index(axis)
    held = [block]
    for step in range(1, count):
        pairs = [(i, (i + step) % count) for i in range(count)]
        held.append(lax.ppermute(block, axis, pairs))
    ordered = []
    for place in range(count):
        chosen = held[0]
        for step in range(1, count):
            chosen = jnp.where(mine == (place + step) % count, held[step], chosen)
        ordered.append(chosen)
    return jnp.stack(ordered, axis=0)


def core_sum(left, right):
    pairs, _, deep, wide, rows = by_seat(left.shape[1])
    mine = lax.axis_index("core")
    away = outer_sum(split_columns(left, 1 - mine), right).astype(jnp.bfloat16)
    other = lax.ppermute(away, "core", [(0, 1), (1, 0)])
    here = outer_sum(split_columns(left, mine), right).astype(jnp.bfloat16)
    both = here.astype(jnp.float32) + other.astype(jnp.float32)
    return both.reshape(pairs, deep, wide, rows, right.shape[1])


def last_sum(blocks):
    return lax.psum_scatter(
        blocks.astype(jnp.bfloat16), "z", scatter_dimension=0, tiled=False
    ).astype(jnp.float32)


def rank_rows(head_ref, dim_ref, lead, head_base, dim_base, ranks, head):
    total = None
    for r in range(ranks):
        row = head_ref[lead + (pl.ds(head_base + r * H + head, 1), slice(None))]
        dims = dim_ref[lead + (slice(dim_base + r * HD, dim_base + (r + 1) * HD), slice(None))]
        term = row * dims
        total = term if total is None else total + term
    return total


def head_pair(head_ref, dim_ref, lead, head_base, dim_base, ranks, pair):
    both = [
        rank_rows(head_ref, dim_ref, lead, head_base, dim_base, ranks, 2 * pair + j)
        * (1.0 / ranks)
        for j in range(2)
    ]
    return jnp.concatenate(both, axis=0)


def stage_factors(every_ref, local_ref, heads, dims):
    chunks = heads.shape[0]
    for c in range(chunks):
        block = local_ref[0] if c == chunks - 1 else every_ref[c, 0]
        dims[c] = block[: 4 * HD].astype(jnp.float32)
        heads[c] = block[4 * HD :].astype(jnp.float32)


def stage_bias(branch_ref, limit_ref, bias):
    chunks, rows = bias.shape[0], bias.shape[1]
    limit = limit_ref[0]
    key = lax.broadcasted_iota(jnp.int32, (rows, rows), 1)
    row = lax.broadcasted_iota(jnp.int32, (rows, rows), 0)
    for c in range(chunks - 1):
        bias[c] = jnp.where(key + c * rows < limit, 0.0, masked_score)
    local = (key <= row) & (key // CONT == row // CONT) & (branch_ref[0] > 0)
    bias[chunks - 1] = jnp.where(local, 0.0, masked_score)


def lane_split(pair_block):
    lane = lax.broadcasted_iota(jnp.int32, pair_block.shape, 1)
    first = jnp.where(lane < HD, pair_block, 0.0)
    second = jnp.where(lane < HD, 0.0, pair_block)
    return jnp.concatenate([first, second], axis=0)


def lane_join(stacked):
    rows = stacked.shape[0] // 2
    lane = lax.broadcasted_iota(jnp.int32, (rows, stacked.shape[1]), 1)
    return jnp.where(lane < HD, stacked[:rows], stacked[rows:])


def diagonal_pair(pair_t):
    row = lax.broadcasted_iota(jnp.int32, pair_t.shape, 0)
    first = jnp.where(row < HD, pair_t, 0.0)
    second = jnp.where(row < HD, 0.0, pair_t)
    return jnp.concatenate([first, second], axis=1)


def dot_nn(left, right):
    return lax.dot_general(
        left, right, (((1,), (0,)), ((), ())), preferred_element_type=jnp.float32
    )


def dot_nt(left, right):
    return lax.dot_general(
        left, right, (((1,), (1,)), ((), ())), preferred_element_type=jnp.float32
    )


def attend_kernel(
    branch_ref, limit_ref, qh_ref, qd_ref, every_ref, local_ref, mixed_ref, log_ref, heads, dims, bias
):
    pair = pl.program_id(1)
    chunks, rows = bias.shape[0], bias.shape[1]

    @pl.when(pair == 0)
    def _():
        stage_factors(every_ref, local_ref, heads, dims)
        stage_bias(branch_ref, limit_ref, bias)
        log_ref[...] = jnp.zeros_like(log_ref)

    query_t = head_pair(qh_ref, qd_ref, (), 0, 0, RQ, pair)
    query = query_t.T.astype(jnp.bfloat16).astype(jnp.float32) * HD ** (-0.5)
    query = lane_split(query).astype(jnp.bfloat16)
    scores = []
    top = None
    for c in range(chunks):
        key_t = head_pair(heads, dims, (c,), 0, 0, RK, pair).astype(jnp.bfloat16)
        score = dot_nn(query, key_t)
        score = score + jnp.concatenate([bias[c], bias[c]], axis=0)
        scores.append(score)
        top = score if top is None else jnp.maximum(top, score)
    top = jnp.max(top, axis=-1, keepdims=True)
    total = None
    mixed = None
    for c in range(chunks):
        value_t = head_pair(heads, dims, (c,), RK * H, RK * HD, RK, pair).astype(jnp.bfloat16)
        weight = jnp.exp(scores[c] - top)
        total = weight if total is None else total + weight
        part = dot_nt(weight.astype(jnp.bfloat16), value_t)
        mixed = part if mixed is None else mixed + part
    total = jnp.sum(total, axis=-1, keepdims=True)
    mixed_ref[0] = lane_join(mixed / total).astype(jnp.bfloat16)
    log_total = top + jnp.log(total)
    lane = lax.broadcasted_iota(jnp.int32, (rows, 128), 1)
    kept = log_ref[0]
    for j in range(2):
        kept = jnp.where(lane == 2 * pair + j, log_total[j * rows : (j + 1) * rows], kept)
    log_ref[0] = kept


def attend_back_kernel(
    branch_ref, limit_ref, qh_ref, qd_ref, every_ref, local_ref, mixed_ref, upstream_ref, log_ref,
    qh_out, qd_out, factor_out, heads, dims, bias, heads_sum, dims_sum,
):
    pair = pl.program_id(1)
    chunks, rows = bias.shape[0], bias.shape[1]

    @pl.when(pair == 0)
    def _():
        stage_factors(every_ref, local_ref, heads, dims)
        stage_bias(branch_ref, limit_ref, bias)
        dims_sum[...] = jnp.zeros_like(dims_sum)
        qd_out[...] = jnp.zeros_like(qd_out)

    query_t = head_pair(qh_ref, qd_ref, (), 0, 0, RQ, pair)
    query_t = query_t.astype(jnp.bfloat16).astype(jnp.float32) * HD ** (-0.5)
    query = lane_split(query_t.T).astype(jnp.bfloat16)
    query_t = diagonal_pair(query_t).astype(jnp.bfloat16)
    upstream = upstream_ref[0].astype(jnp.float32)
    inner = lane_split(upstream * mixed_ref[0].astype(jnp.float32))
    inner = jnp.sum(inner, axis=-1, keepdims=True)
    upstream_t = diagonal_pair(upstream.T).astype(jnp.bfloat16)
    upstream = lane_split(upstream).astype(jnp.bfloat16)
    lane = lax.broadcasted_iota(jnp.int32, (rows, 128), 1)
    log_total = jnp.concatenate(
        [
            jnp.sum(jnp.where(lane == 2 * pair + j, log_ref[0], 0.0), axis=-1, keepdims=True)
            for j in range(2)
        ],
        axis=0,
    )
    query_grad = None
    for c in range(chunks):
        key_t = head_pair(heads, dims, (c,), 0, 0, RK, pair).astype(jnp.bfloat16)
        value_t = head_pair(heads, dims, (c,), RK * H, RK * HD, RK, pair).astype(jnp.bfloat16)
        score = dot_nn(query, key_t)
        score = score + jnp.concatenate([bias[c], bias[c]], axis=0)
        weight = jnp.exp(score - log_total)
        weight_grad = dot_nn(upstream, value_t)
        score_grad = (weight * (weight_grad - inner)).astype(jnp.bfloat16)
        part = dot_nt(score_grad, key_t)
        query_grad = part if query_grad is None else query_grad + part
        key_grad = dot_nn(query_t, score_grad)
        value_grad = dot_nn(upstream_t, weight.astype(jnp.bfloat16))
        for kind, grad in ((0, key_grad), (1, value_grad)):
            for j in range(2):
                half = grad[j * HD : (j + 1) * HD] * (1.0 / RK)
                for r in range(RK):
                    place = kind * RK * H + r * H + 2 * pair + j
                    base = kind * RK * HD + r * HD
                    row = heads[c, pl.ds(place, 1), :]
                    block = dims[c, base : base + HD, :]
                    heads_sum[c, pl.ds(place, 1), :] = jnp.sum(half * block, axis=0, keepdims=True)
                    dims_sum[c, base : base + HD, :] += half * row
    query_grad = (lane_join(query_grad) * (HD ** (-0.5) / RQ)).T
    for j in range(2):
        half = query_grad[j * HD : (j + 1) * HD]
        for r in range(RQ):
            place = r * H + 2 * pair + j
            row = qh_ref[pl.ds(place, 1), :]
            block = qd_ref[r * HD : (r + 1) * HD, :]
            qh_out[pl.ds(place, 1), :] = jnp.sum(half * block, axis=0, keepdims=True)
            qd_out[r * HD : (r + 1) * HD, :] += half * row

    @pl.when(pair == H // 2 - 1)
    def _():
        for c in range(chunks):
            factor_out[c, 0, : 4 * HD] = dims_sum[c].astype(jnp.bfloat16)
            factor_out[c, 0, 4 * HD :] = heads_sum[c].astype(jnp.bfloat16)


def attention_specs(rows, chunks, first):
    width = 4 * HD + 4 * H
    return [
        pl.BlockSpec((1, rows, 1), lambda g, p, *_: (g + first, 0, 0)),
        pl.BlockSpec((RQ * H, rows), lambda g, p, *_: (0, g + first)),
        pl.BlockSpec((RQ * HD, rows), lambda g, p, *_: (0, g + first)),
        pl.BlockSpec((chunks - 1, 1, width, rows), lambda g, p, *_: (0, g + first, 0, 0)),
        pl.BlockSpec((1, width, rows), lambda g, p, *_: (g + first, 0, 0)),
    ]


def attention_scratch(rows, chunks):
    return [
        pltpu.VMEM((chunks, 4 * H, rows), jnp.float32),
        pltpu.VMEM((chunks, 4 * HD, rows), jnp.float32),
        pltpu.VMEM((chunks, rows, rows), jnp.float32),
    ]


def attend(branch, limit, qh, qd, every, local):
    groups_here, _, rows = local.shape
    chunks = PROMPT // rows + 1
    pair_block = pl.BlockSpec((1, rows, 2 * HD), lambda g, p, *_: (g, 0, p))
    work = groups_here * H * rows * rows * chunks
    return pl.pallas_call(
        attend_kernel,
        grid_spec=pltpu.PrefetchScalarGridSpec(
            num_scalar_prefetch=1,
            grid=(groups_here, H // 2),
            in_specs=attention_specs(rows, chunks, 0),
            out_specs=[
                pair_block,
                pl.BlockSpec((1, rows, 128), lambda g, p, *_: (g, 0, 0)),
            ],
            scratch_shapes=attention_scratch(rows, chunks),
        ),
        out_shape=[
            jax.ShapeDtypeStruct((groups_here, rows, H * HD), jnp.bfloat16),
            jax.ShapeDtypeStruct((groups_here, rows, 128), jnp.float32),
        ],
        cost_estimate=pl.CostEstimate(
            flops=work * HD * 8, transcendentals=work, bytes_accessed=8 * 2**20
        ),
        compiler_params=pltpu.CompilerParams(vmem_limit_bytes=56 * 2**20),
        name="attend",
    )(branch, limit, qh, qd, every, local)


def attend_back(branch, limit, qh, qd, every, local, mixed, upstream, log_total, group):
    _, width, rows = local.shape
    chunks = PROMPT // rows + 1
    pair_block = pl.BlockSpec((1, rows, 2 * HD), lambda g, p, *_: (g + group, 0, p))
    work = H * rows * rows * chunks
    return pl.pallas_call(
        attend_back_kernel,
        grid_spec=pltpu.PrefetchScalarGridSpec(
            num_scalar_prefetch=1,
            grid=(1, H // 2),
            in_specs=attention_specs(rows, chunks, group)
            + [
                pair_block,
                pair_block,
                pl.BlockSpec((1, rows, 128), lambda g, p, *_: (g + group, 0, 0)),
            ],
            out_specs=[
                pl.BlockSpec((RQ * H, rows), lambda g, p, *_: (0, g)),
                pl.BlockSpec((RQ * HD, rows), lambda g, p, *_: (0, g)),
                pl.BlockSpec((chunks, 1, width, rows), lambda g, p, *_: (0, g, 0, 0)),
            ],
            scratch_shapes=attention_scratch(rows, chunks)
            + [
                pltpu.VMEM((chunks, 4 * H, rows), jnp.float32),
                pltpu.VMEM((chunks, 4 * HD, rows), jnp.float32),
            ],
        ),
        out_shape=[
            jax.ShapeDtypeStruct((RQ * H, rows), jnp.float32),
            jax.ShapeDtypeStruct((RQ * HD, rows), jnp.float32),
            jax.ShapeDtypeStruct((chunks, 1, width, rows), jnp.bfloat16),
        ],
        cost_estimate=pl.CostEstimate(
            flops=work * HD * 20, transcendentals=work, bytes_accessed=8 * 2**20
        ),
        compiler_params=pltpu.CompilerParams(vmem_limit_bytes=60 * 2**20),
        name="attend_back",
    )(branch, limit, qh, qd, every, local, mixed, upstream, log_total)


def rotate_rows(values, ranks, cosine, sine_part):
    turned = []
    half = HD // 2
    for r in range(ranks):
        first = values[r * HD : r * HD + half]
        second = values[r * HD + half : (r + 1) * HD]
        turned.append(first * cosine - second * sine_part)
        turned.append(second * cosine + first * sine_part)
    return jnp.concatenate(turned, axis=0)


def shards(
    tokens,
    offsets,
    query_head_weight,
    query_dim_weight,
    key_head_weight,
    key_dim_weight,
    value_head_weight,
    value_dim_weight,
    out_weight,
    attention_gain,
    gate_weight,
    up_weight,
    down_weight,
    feedforward_gain,
    cotangent,
):
    every = ("gx", "core", "z", "y")
    packed = jnp.concatenate(
        [
            out_weight,
            key_dim_weight,
            value_dim_weight,
            key_head_weight,
            value_head_weight,
            query_dim_weight,
            query_head_weight,
            attention_gain[:, None],
            feedforward_gain[:, None],
        ],
        axis=1,
    )
    gate_part = shift_gather(gate_weight, "z")
    up_part = shift_gather(up_weight, "z")
    packed_full = lax.all_gather(packed, every, axis=0, tiled=True)
    gate_part, up_part, packed_full = lax.optimization_barrier((gate_part, up_part, packed_full))
    gate_part = double(gate_part, "gx", 0)
    up_part = double(up_part, "y", 1)
    gate_part = double(gate_part, "y", 2)
    up_part = double(up_part, "gx", 0)
    out_full = packed_full[:, :D]
    joined = packed_full[:, D:-2]
    attention_gain_full = packed_full[:, -2]
    feedforward_gain_full = packed_full[:, -1]
    hidden_width = gate_weight.shape[1]
    factor_width = 2 * RK * (HD + H)
    groups_here, rows_here = (tokens.shape[0], tokens.shape[1])
    row_count = groups_here * rows_here
    seat = lax.axis_index(("z", "y"))
    start_row = seat * rows_here
    places = start_row + jnp.arange(rows_here, dtype=jnp.int32)
    in_continuation = places >= PROMPT
    branch_index = jnp.where(in_continuation, (places - PROMPT) // CONT, -1)
    pick_table = (branch_index[:, None] == jnp.arange(NCONT, dtype=jnp.int32)[None, :]).astype(
        jnp.int32
    )
    branch_start = jnp.sum(offsets[:, None, :] * pick_table[None, :, :], axis=-1)
    positions = jnp.where(
        in_continuation[None, :],
        branch_start + ((places - PROMPT) % CONT)[None, :],
        places[None, :],
    ).reshape(row_count)
    limit = jnp.where(in_continuation[None, :], branch_start, places[None, :] + 1)[:, :, None]
    branch = (start_row >= PROMPT).astype(jnp.int32).reshape(1)
    frequency = 10000.0 ** (-2.0 * jnp.arange(HD // 2, dtype=jnp.float32) / HD)
    angles = frequency[:, None] * positions.astype(jnp.float32)[None, :]
    cosine, sine = jnp.cos(angles), jnp.sin(angles)

    flat = tokens.reshape(row_count, D).astype(jnp.float32)
    normed, inverse_first = norm_apply(flat, attention_gain_full.astype(jnp.float32))
    normed_low = normed.astype(jnp.bfloat16)
    projected = lax.dot_general(
        joined, normed_low, (((0,), (1,)), ((), ())), preferred_element_type=jnp.float32
    )
    local = jnp.concatenate(
        [
            rotate_rows(projected[: RK * HD], RK, cosine, sine),
            projected[RK * HD : factor_width],
        ],
        axis=0,
    ).astype(jnp.bfloat16)
    local = local.reshape(factor_width, groups_here, rows_here).transpose(1, 0, 2)
    every_factor = lax.all_gather(local, ("z", "y"), axis=0, tiled=False)
    down_full = lax.all_gather(down_weight, every, axis=0, tiled=True)
    gate_part, up_part, every_factor = lax.optimization_barrier((gate_part, up_part, every_factor))
    gate_full = double(gate_part, "core", 1).reshape(D, hidden_width)
    up_full = double(up_part, "core", 1).reshape(D, hidden_width)
    query_dim = rotate_rows(projected[factor_width : factor_width + RQ * HD], RQ, cosine, sine)
    query_head = projected[factor_width + RQ * HD :]
    mixed, log_total = attend(branch, limit, query_head, query_dim, every_factor, local)
    mixed_flat = mixed.reshape(row_count, H * HD)
    middle = flat + jnp.dot(mixed_flat, out_full, preferred_element_type=jnp.float32)
    normed_second, inverse_second = norm_apply(middle, feedforward_gain_full.astype(jnp.float32))
    second_low = normed_second.astype(jnp.bfloat16)
    gate = jnp.dot(second_low, gate_full, preferred_element_type=jnp.float32)
    upper = jnp.dot(second_low, up_full, preferred_element_type=jnp.float32)
    gate_sigmoid = jax.nn.sigmoid(gate)
    swish = gate * gate_sigmoid
    hidden = (swish * upper).astype(jnp.bfloat16)
    result = middle + jnp.dot(hidden, down_full, preferred_element_type=jnp.float32)
    output = result.astype(jnp.bfloat16).reshape(groups_here, rows_here, D)
    upstream = cotangent.reshape(row_count, D).astype(jnp.float32)
    upstream_low = upstream.astype(jnp.bfloat16)
    half_width = D // 2
    down_sums = []
    for side in range(2):
        partial_sum = outer_sum(hidden, upstream_low[:, side * half_width : (side + 1) * half_width])
        partial_sum = partial_sum.astype(jnp.bfloat16).reshape(*by_seat(hidden_width), half_width)
        down_sums.append(halve(partial_sum, "core", 1))
    hidden_grad = times_transposed(upstream_low, down_full)
    up_rows = (hidden_grad * swish).astype(jnp.bfloat16)
    gate_rows = (hidden_grad * upper * gate_sigmoid * (1.0 + gate * (1.0 - gate_sigmoid))).astype(
        jnp.bfloat16
    )
    gate_sum = core_sum(second_low, gate_rows)
    up_sum = core_sum(second_low, up_rows)
    second_grad = times_transposed(gate_rows, gate_full) + times_transposed(up_rows, up_full)
    middle_part, feedforward_gain_grad = norm_back(
        middle, inverse_second, feedforward_gain_full.astype(jnp.float32), second_grad
    )
    middle_grad = upstream + middle_part
    branch_low = middle_grad.astype(jnp.bfloat16)
    out_sum = to_seat(core_sum(mixed_flat, branch_low), True)
    mixed_grad = (
        times_transposed(branch_low, out_full)
        .astype(jnp.bfloat16)
        .reshape(groups_here, rows_here, H * HD)
    )
    for side in range(2):
        down_sums[side], mixed_grad = first_step(down_sums[side], side == 0, mixed_grad)
    gate_sum, mixed_grad = first_step(gate_sum, True, mixed_grad)
    up_sum, mixed_grad = first_step(up_sum, False, mixed_grad)
    prompt_seats = PROMPT // rows_here
    deep, wide = lax.axis_size("z"), lax.axis_size("y")
    query_head_grad, query_dim_grad, summed = [], [], []
    for group in range(groups_here):
        if group == groups_here - 1:
            for side in range(2):
                down_sums[side], mixed_grad = second_step(down_sums[side], side == 0, mixed_grad)
        head_part, dim_part, factor_part = attend_back(
            branch,
            limit,
            query_head,
            query_dim,
            every_factor,
            local,
            mixed,
            mixed_grad,
            log_total,
            group,
        )
        query_head_grad.append(head_part)
        query_dim_grad.append(dim_part)
        prompt_part = factor_part[:prompt_seats].reshape(
            prompt_seats // wide, wide, factor_width, rows_here
        )
        if group < groups_here - 1:
            prompt_sum, mixed_grad = halve(prompt_part, "y", 1, mixed_grad)
        else:
            prompt_sum = halve(prompt_part, "y", 1)
        prompt_sum = shift_sum(prompt_sum, "z", prompt_seats // wide)
        summed.append(
            jnp.where(branch[0] > 0, factor_part[prompt_seats, 0].astype(jnp.float32), prompt_sum)
        )
    gate_sum = second_step(gate_sum, True)
    up_sum = second_step(up_sum, False)
    query_head_grad = jnp.concatenate(query_head_grad, axis=1)
    query_dim_grad = jnp.concatenate(query_dim_grad, axis=1)
    summed = jnp.concatenate(summed, axis=1)
    summed = summed.astype(jnp.bfloat16).astype(jnp.float32)
    factor_grad = jnp.concatenate(
        [
            rotate_rows(summed[: RK * HD], RK, cosine, -sine),
            summed[RK * HD :],
            rotate_rows(query_dim_grad, RQ, cosine, -sine),
            query_head_grad,
        ],
        axis=0,
    ).astype(jnp.bfloat16)
    first_grad = lax.dot_general(
        factor_grad, joined, (((0,), (1,)), ((), ())), preferred_element_type=jnp.float32
    )
    input_part, attention_gain_grad = norm_back(
        flat, inverse_first, attention_gain_full.astype(jnp.float32), first_grad
    )
    input_gradient = (
        (middle_grad + input_part).astype(jnp.bfloat16).reshape(groups_here, rows_here, D)
    )
    joined_grad = lax.dot_general(
        normed_low, factor_grad, (((0,), (1,)), ((), ())), preferred_element_type=jnp.float32
    )
    joined_sum = jnp.concatenate(
        [joined_grad, attention_gain_grad[:, None], feedforward_gain_grad[:, None]], axis=1
    )
    joined_sum = joined_sum.astype(jnp.bfloat16).reshape(*by_seat(D), -1)
    joined_sum = to_seat(halve(joined_sum, "core", 1), True)
    joined_out = shift_sum(joined_sum, "z", deep)
    down_out = last_sum(jnp.concatenate(down_sums, axis=2))
    big_out = last_sum(jnp.concatenate([gate_sum, up_sum, out_sum], axis=2))
    gate_out = big_out[:, :hidden_width]
    up_out = big_out[:, hidden_width : 2 * hidden_width]
    out_weight_out = big_out[:, 2 * hidden_width :]
    widths = [RK * HD, RK * HD, RK * H, RK * H, RQ * HD, RQ * H, 1, 1]
    cuts = [sum(widths[: index + 1]) for index in range(len(widths) - 1)]
    pieces = jnp.split(joined_out, cuts, axis=1)
    return (
        output,
        input_gradient,
        pieces[5],
        pieces[4],
        pieces[2],
        pieces[0],
        pieces[3],
        pieces[1],
        out_weight_out,
        pieces[6][:, 0],
        gate_out,
        up_out,
        down_out,
        pieces[7][:, 0],
    )


def solution(mesh):
    groups, seats = mesh.shape["grp"], mesh.shape["seq"]
    fine = jax.sharding.Mesh(
        mesh.devices.reshape(groups // 2, 2, seats // 2, 2), ("gx", "core", "z", "y")
    )
    grp, seq = ("gx", "core"), ("z", "y")
    token = P(grp, seq, None)
    weight = P(grp + seq, None)
    gain = P(grp + seq)
    placed = (token, P(grp, None)) + (weight,) * 7 + (gain,) + (weight,) * 3 + (gain, token)

    return jax.shard_map(
        shards,
        mesh=fine,
        in_specs=placed,
        out_specs=(token, token) + (weight,) * 7 + (gain,) + (weight,) * 3 + (gain,),
        check_vma=False,
    )
```
